256 devices in a mesh: row: 32 (over z_hi, y, core), col: 8 (over z_lo, x).
Axes of the slice: x: 4, y: 4, z: 8 (z_hi: 4, z_lo: 2; z = z_hi * 2 + z_lo), core: 2. Of those that a mesh axis runs over, the one named last changes fastest.
Arguments:
- matrix: float32 [16384, 16384], P('row', 'col'), as said below
- inverse_blocks: float32 [2, 256, 256], replicated, as said below
- pivots: int32 [512], replicated, may hold values from 0 to 16383, as said below
Outputs:
- updated: float32 [16384, 16384], P('row', 'col')
- factor: float32 [16384, 512], P('row')
The draws below stay inside these ranges and needn't reach their ends.
Inputs may be any that keep to these rules, and one draw needn't show every extreme that they name: matrix is exactly symmetric. `inverse_blocks`: each block is exactly symmetric. pivots[i] is i or at least 512; the entries of at least 512 are distinct; pivots[0] is 0; the last entry is 16383.
All inputs are finite; a program needn't handle non-finite values.
Results may differ from the reference program's by a relative error of at most 0.00018.
Values sent between devices are 32-bit elements; how exact they have to be, the bound alone decides.
A program may use at most 64 MiB of HBM per device.

```python
import jax
import jax.numpy as jnp
from jax import lax

N = 16384
NB = 256


def draw_matrix(key, part):
    key_raw = jax.random.fold_in(key, 0)
    raw = jax.random.normal(key_raw, (N, N), jnp.float32)
    return (raw + raw.T) * 0.7071


def draw_inverse_blocks(key, part):
    key_off, key_diag, key_sign = jax.random.split(key, 3)
    offdiag = jax.random.normal(key_off, (2, NB, NB), jnp.float32) * 0.004
    offdiag = (offdiag + jnp.swapaxes(offdiag, 1, 2)) * 0.7071
    signs = jnp.where(jax.random.randint(key_sign, (2, NB), 0, 2) == 0, -1.0, 1.0)
    diagonal = jax.random.uniform(key_diag, (2, NB), jnp.float32, 0.1, 0.3) * signs
    identity = jnp.eye(NB, dtype=jnp.float32)
    return offdiag * (1.0 - identity) + diagonal[:, :, None] * identity


def draw_pivots(key, part):
    key_perm, key_flag = jax.random.split(key)
    lower = jax.random.permutation(key_perm, N - 2 * NB - 1)[:2 * NB - 1]
    top_value = jnp.array([N - 2 * NB - 1], dtype=lower.dtype)
    targets = jnp.concatenate([lower, top_value]) + 2 * NB
    flags = jax.random.randint(key_flag, (2 * NB,), 0, 2)
    flags = flags.at[0].set(0)
    flags = flags.at[2 * NB - 1].set(1)
    return jnp.where(flags == 1, targets, jnp.arange(2 * NB)).astype(jnp.int32)


def setup_inputs(seed: int = 0) -> dict:
    arg_keys = jax.random.split(jax.random.key(seed), 4)
    return {
        "matrix": draw_matrix(jax.random.fold_in(arg_keys[3], 71), 0),
        "inverse_blocks": draw_inverse_blocks(jax.random.fold_in(arg_keys[3], 71), 0),
        "pivots": draw_pivots(jax.random.fold_in(arg_keys[3], 71), 0),
    }


def product(left, right):
    return jnp.dot(left, right, precision=lax.Precision.HIGHEST, preferred_element_type=jnp.float32)


def outside(indices, chosen):
    return 1.0 - jnp.any(indices[:, None] == chosen[None, :], axis=1).astype(jnp.float32)


def reference(matrix, inverse_blocks, pivots):
    first_pivots = pivots[:NB]
    second_pivots = pivots[NB:]
    indices = jnp.arange(N, dtype=jnp.int32)
    live_one = outside(indices, first_pivots)
    live_two = outside(indices, pivots)
    panel_one = jnp.take(matrix, first_pivots, axis=1)
    factor_one = product(panel_one, inverse_blocks[0])
    shrunk = matrix - (live_one[:, None] * live_one[None, :]) * product(factor_one, panel_one.T)
    corner = jnp.take(panel_one, second_pivots, axis=0)
    panel_two = jnp.take(matrix, second_pivots, axis=1) - live_one[:, None] * product(factor_one, corner.T)
    factor_two = product(panel_two, inverse_blocks[1])
    updated = shrunk - (live_two[:, None] * live_two[None, :]) * product(factor_two, panel_two.T)
    factor = jnp.concatenate([live_one[:, None] * factor_one, live_two[:, None] * factor_two], axis=1)
    return (updated, factor)
```

```python
import jax
import jax.numpy as jnp
from jax import lax
from jax.experimental import pallas as pl
from jax.experimental.pallas import tpu as pltpu
from jax.sharding import PartitionSpec as P

MESH = pl.DeviceIdType.MESH
F32, BF16 = jnp.float32, jnp.bfloat16
ROWS, COLS, NB, NP = 512, 2048, 256, 512
PARTS, LANES = 4, 128
PIECE, EXTRA = 64, 16
SLICE = PIECE + EXTRA
ORDERS = (("xa", "xb", "zl"), ("xb", "xa", "zl"), ("zl", "xa", "xb"), ("zl", "xb", "xa"))
Z_ORDERS = (("za", "zb"), ("zb", "za"), ("za", "zb"), ("zb", "za"))
Y_ORDERS = (("ya", "yb"), ("yb", "ya"), ("yb", "ya"), ("ya", "yb"))
CORNER_ORDER = ("xa", "xb", "zl")
CORNER_SUM = ("co", "ya", "yb", "za", "zb")


def flip_a(v):
    return v + 1 - 2 * (v % 2)


def flip_b(v):
    return (v + 2 * (v % 2) + 3) % 4


def bit_a(v):
    return ((v + 1) // 2) % 2


def bit_b(v):
    return v // 2


def target_bits(s):
    x, zl = s % 4, s // 4
    return {"xa": bit_a(x), "xb": bit_b(x), "zl": zl}


def slot_of(order, s):
    b = target_bits(s)
    return b[order[0]] * 4 + b[order[1]] * 2 + b[order[2]]


def split(a):
    hi = a.astype(BF16)
    return hi, (a - hi.astype(F32)).astype(BF16)


def dot(a, b, dims):
    return lax.dot_general(a, b, (dims, ((), ())), preferred_element_type=F32)


def dot3(a, b, dims):
    (ah, al), (bh, bl) = a, b
    return dot(ah, bh, dims) + (dot(ah, bl, dims) + dot(al, bh, dims))


NN = ((1,), (0,))
NT = ((1,), (1,))
TN = ((0,), (0,))


def select_kernel(pivots_ref, m_ref, out_ref, acc):
    k = pl.program_id(0)
    row_start = lax.axis_index("row") * ROWS
    width = m_ref.shape[1]
    col_start = lax.axis_index("col") * COLS + k * width
    pivots = pivots_ref[...]
    ids = lax.broadcasted_iota(jnp.int32, (width, NP), 0) + col_start
    onehot = (ids == pivots).astype(F32).astype(BF16)
    hi, lo = split(m_ref[...])
    part = dot(hi, onehot, NN) + dot(lo, onehot, NN)

    @pl.when(k == 0)
    def _():
        acc[...] = part

    @pl.when(k > 0)
    def _():
        acc[...] += part

    @pl.when(k == pl.num_programs(0) - 1)
    def _():
        rows = lax.broadcasted_iota(jnp.int32, (ROWS, NB), 0) + row_start
        chosen = (rows == pivots[:, NB:]).astype(F32).astype(BF16)
        hi, lo = split(acc[:, :NB])
        corner = dot(chosen, hi, TN) + dot(chosen, lo, TN)
        for p in range(PARTS):
            for s in range(8):
                at = slot_of(ORDERS[p], s) * SLICE
                out_ref[p, at : at + PIECE, :] = acc[
                    s * PIECE : (s + 1) * PIECE, p * LANES : (p + 1) * LANES
                ]
                first = (p // 2) * 128 + s * EXTRA
                lane = (p % 2) * LANES
                out_ref[p, at + PIECE : at + SLICE, :] = corner[
                    first : first + EXTRA, lane : lane + LANES
                ]


def exchange_kernel(
    s_ref, c_ref, r_ref, k_ref, rx, sum_one, sum_two, q, ar, arx, send_sem, recv_sem, own_sem
):
    row, col = lax.axis_index("row"), lax.axis_index("col")
    zh, y, core = row // 8, (row % 8) // 2, row % 2
    zl, x = col // 4, col % 4
    bits = {"xa": bit_a(x), "xb": bit_b(x), "zl": zl}

    def device(zh_, y_, core_, zl_, x_):
        return (zh_ * 8 + y_ * 2 + core_, zl_ * 4 + x_)

    def storage(zh_, y_, core_):
        return y_ * 8 + core_ * 4 + zh_

    partner = {
        "xa": device(zh, y, core, zl, flip_a(x)),
        "xb": device(zh, y, core, zl, flip_b(x)),
        "zl": device(zh, y, core, 1 - zl, x),
        "za": device(flip_a(zh), y, core, zl, x),
        "zb": device(flip_b(zh), y, core, zl, x),
        "ya": device(zh, flip_a(y), core, zl, x),
        "yb": device(zh, flip_b(y), core, zl, x),
        "co": device(zh, y, 1 - core, zl, x),
    }
    flipped = {
        "za": flip_a(zh),
        "zb": flip_b(zh),
        "ya": flip_a(y),
        "yb": flip_b(y),
        "zz": (zh + 2) % 4,
        "yy": (y + 2) % 4,
    }
    dest = device(zl * 2 + x % 2, (y % 2) * 2 + x // 2, core, zh // 2, (zh % 2) * 2 + y // 2)
    dest_slot = storage(zl * 2 + x % 2, (y % 2) * 2 + x // 2, core)
    source = device(zl * 2 + x // 2, (x % 2) * 2 + y // 2, core, zh // 2, (y % 2) * 2 + zh % 2)
    is_self = (dest[0] == row) & (dest[1] == col)
    not_self = jnp.logical_not(is_self)

    barrier = pltpu.get_barrier_semaphore()

    def greet(dev):
        pl.semaphore_signal(barrier, inc=1, device_id=dev, device_id_type=MESH)

    for dev in partner.values():
        greet(dev)

    @pl.when(not_self)
    def _():
        greet(dest)
        greet(source)
        pl.semaphore_wait(barrier, len(partner) + 2)

    @pl.when(is_self)
    def _():
        pl.semaphore_wait(barrier, len(partner))

    ids = {}
    sent = []

    def copy(key, src, dst, dev):
        n = ids.setdefault(key, len(ids))
        return pltpu.make_async_remote_copy(
            src_ref=src,
            dst_ref=dst,
            send_sem=send_sem.at[n],
            recv_sem=recv_sem.at[n],
            device_id=dev,
            device_id_type=MESH,
        )

    def send(key, src, dst, dim):
        c = copy(key, src, dst, partner[dim])
        c.start()
        sent.append(c)

    def arrive(key, dst, dim):
        copy(key, dst, dst, partner[dim]).wait_recv()

    def at(ref, p, start, size):
        return ref.at[p, pl.ds(pl.multiple_of(start, 8), size), :]

    def load(ref, p, start, size):
        return ref[p, pl.ds(pl.multiple_of(start, 8), size), :]

    R1, R2, R3 = 4 * SLICE, 2 * SLICE, SLICE

    def rx_at(p, n):
        return rx.at[p, (0, R1, R1 + R2)[n] : (R1, R1 + R2, R1 + R2 + R3)[n], :]

    for p in range(PARTS):
        d = ORDERS[p][0]
        send(("rs0", p), at(s_ref, p, (1 - bits[d]) * R1, R1), rx_at(p, 0), d)
    for p in range(PARTS):
        d, e = ORDERS[p][:2]
        arrive(("rs0", p), rx_at(p, 0), d)
        sum_one[p] = load(s_ref, p, bits[d] * R1, R1) + rx[p, :R1, :]
        send(("rs1", p), at(sum_one, p, (1 - bits[e]) * R2, R2), rx_at(p, 1), e)
    for p in range(PARTS):
        d, e = ORDERS[p][1:]
        arrive(("rs1", p), rx_at(p, 1), d)
        sum_two[p] = load(sum_one, p, bits[d] * R2, R2) + rx[p, R1 : R1 + R2, :]
        send(("rs2", p), at(sum_two, p, (1 - bits[e]) * R3, R3), rx_at(p, 2), e)

    mine = storage(zh, y, core)

    def c_at(p, slot, count):
        return at(c_ref, p, slot * PIECE, count * PIECE)

    def place(p):
        return copy(("place", p), q.at[p, :PIECE, :], c_at(p, dest_slot, 1), dest)

    def keep(p):
        return pltpu.make_async_copy(q.at[p, :PIECE, :], c_at(p, dest_slot, 1), own_sem.at[p])

    def r_slot(p):
        a, b, c = ORDERS[p]
        return bits[a] * 4 + bits[b] * 2 + bits[c]

    def r_at(p, slot, count):
        return at(r_ref, p, slot * PIECE, count * PIECE)

    for p in range(PARTS):
        d = ORDERS[p][2]
        arrive(("rs2", p), rx_at(p, 2), d)
        q[p] = load(sum_two, p, bits[d] * R3, R3) + rx[p, R1 + R2 :, :]

        @pl.when(not_self)
        def _(p=p):
            place(p).start()

        @pl.when(is_self)
        def _(p=p):
            keep(p).start()

        r_ref[p, pl.ds(pl.multiple_of(r_slot(p) * PIECE, 8), PIECE), :] = q[p, :PIECE, :]
        send(("r0", p), q.at[p, :PIECE, :], r_at(p, r_slot(p), 1), d)
        ar[0, p * EXTRA : (p + 1) * EXTRA, :] = q[p, PIECE:, :]

    def corner_send(n):
        send(("ar", n), ar.at[n], arx.at[n], CORNER_SUM[n])

    def corner_add(n):
        arrive(("ar", n), arx.at[n], CORNER_SUM[n])
        ar[n + 1] = ar[n] + arx[n]

    corner_send(0)

    for p in range(PARTS):

        @pl.when(not_self)
        def _(p=p):
            copy(("place", p), c_at(p, mine, 1), c_at(p, mine, 1), source).wait_recv()

        @pl.when(is_self)
        def _(p=p):
            keep(p).wait()

        z0, z1 = Z_ORDERS[p]
        send(("z0", p), c_at(p, mine, 1), c_at(p, mine, 1), z0)
        send(("z1", p), c_at(p, mine, 1), c_at(p, mine, 1), z1)
        if p == 0:
            corner_add(0)
            corner_send(1)

    for p in range(PARTS):
        z0, z1 = Z_ORDERS[p]
        near = storage(flipped[z0], y, core)
        arrive(("z0", p), c_at(p, near, 1), z0)
        send(("z2", p), c_at(p, near, 1), c_at(p, near, 1), z1)
    corner_add(1)
    corner_send(2)

    group = storage(0, y, core)
    for p in range(PARTS):
        z0, z1 = Z_ORDERS[p]
        arrive(("z1", p), c_at(p, storage(flipped[z1], y, core), 1), z1)
        arrive(("z2", p), c_at(p, storage(flipped["zz"], y, core), 1), z1)
        y0, y1 = Y_ORDERS[p]
        send(("y0", p), c_at(p, group, 4), c_at(p, group, 4), y0)
        send(("y1", p), c_at(p, group, 4), c_at(p, group, 4), y1)
        send(("c0", p), c_at(p, group, 4), c_at(p, group, 4), "co")
        a, b, c = ORDERS[p]
        arrive(("r0", p), r_at(p, bits[a] * 4 + bits[b] * 2 + 1 - bits[c], 1), c)
        pair = bits[a] * 4 + bits[b] * 2
        send(("r1", p), r_at(p, pair, 2), r_at(p, pair, 2), b)
        if p == 1:
            corner_add(2)
            corner_send(3)
    corner_add(3)
    corner_send(4)

    for p in range(PARTS):
        y0, y1 = Y_ORDERS[p]
        near = storage(0, flipped[y0], core)
        arrive(("y0", p), c_at(p, near, 4), y0)
        send(("y2", p), c_at(p, near, 4), c_at(p, near, 4), y1)
        send(("c1", p), c_at(p, near, 4), c_at(p, near, 4), "co")
        a, b, c = ORDERS[p]
        arrive(("r1", p), r_at(p, bits[a] * 4 + (1 - bits[b]) * 2, 2), b)
        send(("r2", p), r_at(p, bits[a] * 4, 4), r_at(p, bits[a] * 4, 4), a)
        if p == 0:
            corner_add(4)
            ka, kb, kc = CORNER_ORDER
            k0 = bits[ka] * 4 + bits[kb] * 2 + bits[kc]
            k_ref[pl.ds(k0, 1)] = ar[5][None]
            send(("k0",), ar.at[5], k_ref.at[k0], kc)
        if p == 3:
            arrive(("k0",), k_ref.at[bits[ka] * 4 + bits[kb] * 2 + 1 - bits[kc]], kc)
            two = k_ref.at[pl.ds(bits[ka] * 4 + bits[kb] * 2, 2)]
            send(("k1",), two, two, kb)

    for p in range(PARTS):
        y0, y1 = Y_ORDERS[p]
        near = storage(0, flipped[y1], core)
        arrive(("y1", p), c_at(p, near, 4), y1)
        send(("c2", p), c_at(p, near, 4), c_at(p, near, 4), "co")
        if p == 1:
            arrive(("k1",), k_ref.at[pl.ds(bits[ka] * 4 + (1 - bits[kb]) * 2, 2)], kb)
            four = k_ref.at[pl.ds(bits[ka] * 4, 4)]
            send(("k2",), four, four, ka)

    for p in range(PARTS):
        far = storage(0, flipped["yy"], core)
        arrive(("y2", p), c_at(p, far, 4), Y_ORDERS[p][1])
        send(("c3", p), c_at(p, far, 4), c_at(p, far, 4), "co")

    arrive(("k2",), k_ref.at[pl.ds((1 - bits[ka]) * 4, 4)], ka)
    for p in range(PARTS):
        a = ORDERS[p][0]
        arrive(("r2", p), r_at(p, (1 - bits[a]) * 4, 4), a)
        y0, y1 = Y_ORDERS[p]
        arrive(("c0", p), c_at(p, storage(0, y, 1 - core), 4), "co")
        arrive(("c1", p), c_at(p, storage(0, flipped[y0], 1 - core), 4), "co")
        arrive(("c2", p), c_at(p, storage(0, flipped[y1], 1 - core), 4), "co")
        arrive(("c3", p), c_at(p, storage(0, flipped["yy"], 1 - core), 4), "co")

    @pl.when(not_self)
    def _():
        for p in range(PARTS):
            place(p).wait_send()

    for c in sent:
        c.wait_send()


MESSAGES = 3 * PARTS + PARTS + 3 * PARTS + 3 * PARTS + 4 * PARTS + 3 * PARTS + 5 + 3


def live(ids, chosen):
    hit = jnp.max((ids == chosen).astype(F32), axis=1, keepdims=True)
    return 1.0 - hit


def update_kernel(
    pivots_ref, m_ref, w_ref, k_ref, r_ref, c_ref, out_ref, factor_ref, left_hi, left_lo, t_hi, t_lo
):
    j = pl.program_id(0)
    pivots = pivots_ref[...]

    @pl.when(j == 0)
    def _():
        slots = [slot_of(CORNER_ORDER, s) for s in range(8)]
        corner = jnp.concatenate(
            [
                jnp.concatenate(
                    [
                        k_ref[slots[s], (2 * half + h) * EXTRA : (2 * half + h + 1) * EXTRA, :]
                        for h in range(2)
                    ],
                    axis=1,
                )
                for half in range(2)
                for s in range(8)
            ],
            axis=0,
        )
        w_one, w_two = split(w_ref[0]), split(w_ref[1])
        t = split(dot3(w_one, split(corner), NT))
        t_hi[...], t_lo[...] = t
        rows = []
        for p in range(PARTS):
            rows.append(
                jnp.concatenate(
                    [
                        r_ref[p, slot * PIECE : (slot + 1) * PIECE, :]
                        for slot in (slot_of(ORDERS[p], s) for s in range(8))
                    ],
                    axis=0,
                )
            )
        one = jnp.concatenate(rows[:2], axis=1)
        two = jnp.concatenate(rows[2:], axis=1)
        ids = lax.axis_index("row") * ROWS
        ids_one = ids + lax.broadcasted_iota(jnp.int32, (ROWS, NB), 0)
        live_one = live(ids_one, pivots[:, :NB])
        live_two = live_one * live(ids_one, pivots[:, NB:])
        one = split(one)
        factor_one = live_one * dot3(one, w_one, NN)
        two = two - live_one * dot3(one, t, NN)
        factor_two = live_two * dot3(split(two), w_two, NN)
        factor_ref[:, :NB] = factor_one
        factor_ref[:, NB:] = factor_two
        left_hi[:, :NB], left_lo[:, :NB] = split(factor_one)
        left_hi[:, NB:], left_lo[:, NB:] = split(factor_two)

    base = (j // 2) * 16 + (j % 2) * 4

    def piece(p, s):
        slot = base + ((s % 4) // 2) * 8 + (s // 4) * 2 + s % 2
        return c_ref[p, pl.ds(pl.multiple_of(slot * PIECE, 8), PIECE), :]

    def panel(n):
        return jnp.concatenate(
            [
                jnp.concatenate([piece(2 * n, s), piece(2 * n + 1, s)], axis=1)
                for s in range(8)
            ],
            axis=0,
        )

    width = m_ref.shape[1]
    ids = lax.axis_index("col") * COLS + j * width
    ids = ids + lax.broadcasted_iota(jnp.int32, (width, NB), 0)
    live_one = live(ids, pivots[:, :NB])
    live_two = live_one * live(ids, pivots[:, NB:])
    one = live_one * panel(0)
    one_hi, one_lo = split(one)
    two = live_two * (panel(1) - dot3((one_hi, one_lo), (t_hi[...], t_lo[...]), NN))
    two_hi, two_lo = split(two)
    right = (
        jnp.concatenate([one_hi, two_hi], axis=1),
        jnp.concatenate([one_lo, two_lo], axis=1),
    )
    out_ref[...] = m_ref[...] - dot3((left_hi[...], left_lo[...]), right, NT)


def shards(matrix, inverse_blocks, pivots):
    pivots = pivots.reshape(1, NP)
    whole = lambda shape: pl.BlockSpec(
        shape, lambda *_: (0,) * len(shape), pipeline_mode=pl.Buffered(1)
    )
    picked = pl.pallas_call(
        select_kernel,
        name="select",
        grid=(4,),
        out_shape=jax.ShapeDtypeStruct((PARTS, 8 * SLICE, LANES), F32),
        in_specs=[whole((1, NP)), pl.BlockSpec((ROWS, 512), lambda k: (0, k))],
        out_specs=whole((PARTS, 8 * SLICE, LANES)),
        scratch_shapes=[pltpu.VMEM((ROWS, NP), F32)],
    )(pivots, matrix)
    vmem = pl.BlockSpec(memory_space=pltpu.VMEM)
    across, rows, corner = pl.pallas_call(
        exchange_kernel,
        name="exchange",
        out_shape=(
            jax.ShapeDtypeStruct((PARTS, COLS, LANES), F32),
            jax.ShapeDtypeStruct((PARTS, ROWS, LANES), F32),
            jax.ShapeDtypeStruct((8, PARTS * EXTRA, LANES), F32),
        ),
        in_specs=[vmem],
        out_specs=(vmem, vmem, vmem),
        scratch_shapes=[
            pltpu.VMEM((PARTS, 7 * SLICE, LANES), F32),
            pltpu.VMEM((PARTS, 4 * SLICE, LANES), F32),
            pltpu.VMEM((PARTS, 2 * SLICE, LANES), F32),
            pltpu.VMEM((PARTS, SLICE, LANES), F32),
            pltpu.VMEM((6, PARTS * EXTRA, LANES), F32),
            pltpu.VMEM((5, PARTS * EXTRA, LANES), F32),
            pltpu.SemaphoreType.DMA((MESSAGES,)),
            pltpu.SemaphoreType.DMA((MESSAGES,)),
            pltpu.SemaphoreType.DMA((PARTS,)),
        ],
        compiler_params=pltpu.CompilerParams(
            collective_id=0, has_side_effects=True, vmem_limit_bytes=40 << 20
        ),
    )(picked)
    return tuple(
        pl.pallas_call(
            update_kernel,
            name="update",
            grid=(4,),
            out_shape=(
                jax.ShapeDtypeStruct((ROWS, COLS), F32),
                jax.ShapeDtypeStruct((ROWS, NP), F32),
            ),
            in_specs=[
                whole((1, NP)),
                pl.BlockSpec((ROWS, 512), lambda j: (0, j)),
                whole((2, NB, NB)),
                whole((8, PARTS * EXTRA, LANES)),
                whole((PARTS, ROWS, LANES)),
                whole((PARTS, COLS, LANES)),
            ],
            out_specs=(
                pl.BlockSpec((ROWS, 512), lambda j: (0, j)),
                whole((ROWS, NP)),
            ),
            scratch_shapes=[
                pltpu.VMEM((ROWS, NP), BF16),
                pltpu.VMEM((ROWS, NP), BF16),
                pltpu.VMEM((NB, NB), BF16),
                pltpu.VMEM((NB, NB), BF16),
            ],
            compiler_params=pltpu.CompilerParams(vmem_limit_bytes=40 << 20),
        )(pivots, matrix, inverse_blocks, corner, rows, across)
    )


def solution(mesh):
    return jax.shard_map(
        shards,
        mesh=mesh,
        in_specs=(P("row", "col"), P(), P()),
        out_specs=(P("row", "col"), P("row", None)),
        check_vma=False,
    )
```

```python
import jax
import jax.numpy as jnp
from jax import lax
from jax.experimental import pallas as pl
from jax.experimental.pallas import tpu as pltpu
from jax.sharding import PartitionSpec as P

MESH = pl.DeviceIdType.MESH
F32, BF16 = jnp.float32, jnp.bfloat16
ROWS, COLS, NB, NP = 512, 2048, 256, 512
PARTS, LANES = 4, 128
PIECE = 64
CORNER = PARTS
ORDERS = (
    ("xa", "xb", "zl"),
    ("xb", "xa", "zl"),
    ("xa", "xb", "zl"),
    ("xb", "xa", "zl"),
    ("zl", "xa", "xb"),
)
Z_ORDERS = (("za", "zb"), ("zb", "za"), ("za", "zb"), ("zb", "za"))
Y_ORDERS = (("ya", "yb"), ("yb", "ya"), ("yb", "ya"), ("ya", "yb"))
CORNER_SUM = (("ya", "yb", "yf"), ("za", "zb", "zf"), ("co",))


def flip_a(v):
    return v + 1 - 2 * (v % 2)


def flip_b(v):
    return (v + 2 * (v % 2) + 3) % 4


def bit_a(v):
    return ((v + 1) // 2) % 2


def bit_b(v):
    return v // 2


def target_bits(s):
    x, zl = s % 4, s // 4
    return {"xa": bit_a(x), "xb": bit_b(x), "zl": zl}


def slot_of(order, s):
    b = target_bits(s)
    return b[order[0]] * 4 + b[order[1]] * 2 + b[order[2]]


def split(a):
    hi = a.astype(BF16)
    return hi, (a - hi.astype(F32)).astype(BF16)


def dot(a, b, dims):
    return lax.dot_general(a, b, (dims, ((), ())), preferred_element_type=F32)


def dot3(a, b, dims):
    (ah, al), (bh, bl) = a, b
    return dot(ah, bh, dims) + (dot(ah, bl, dims) + dot(al, bh, dims))


NN = ((1,), (0,))
NT = ((1,), (1,))
TN = ((0,), (0,))


def source_slot(s):
    return (s % 4) * 2 + s // 4


def live(ids, chosen):
    hit = jnp.max((ids == chosen).astype(F32), axis=1, keepdims=True)
    return 1.0 - hit


def panels_kernel(
    pivots_ref,
    w_ref,
    m_hbm,
    out_ref,
    factor_ref,
    m_ref,
    onehot,
    s_ref,
    rx,
    sum_one,
    half,
    q,
    c_ref,
    r_ref,
    k_ref,
    ar,
    arx,
    left_hi,
    left_lo,
    t_hi,
    t_lo,
    send_sem,
    recv_sem,
    own_sem,
    load_sem,
):
    row, col = lax.axis_index("row"), lax.axis_index("col")
    zh, y, core = row // 8, (row % 8) // 2, row % 2
    zl, x = col // 4, col % 4
    bits = {"xa": bit_a(x), "xb": bit_b(x), "zl": zl}

    def device(zh_, y_, core_, zl_, x_):
        return (zh_ * 8 + y_ * 2 + core_, zl_ * 4 + x_)

    def storage(zh_, y_, core_):
        return y_ * 8 + core_ * 4 + zh_

    partner = {
        "xa": device(zh, y, core, zl, flip_a(x)),
        "xb": device(zh, y, core, zl, flip_b(x)),
        "xf": device(zh, y, core, zl, (x + 2) % 4),
        "zl": device(zh, y, core, 1 - zl, x),
        "zf": device((zh + 2) % 4, y, core, zl, x),
        "yf": device(zh, (y + 2) % 4, core, zl, x),
        "za": device(flip_a(zh), y, core, zl, x),
        "zb": device(flip_b(zh), y, core, zl, x),
        "ya": device(zh, flip_a(y), core, zl, x),
        "yb": device(zh, flip_b(y), core, zl, x),
        "co": device(zh, y, 1 - core, zl, x),
    }
    flipped = {
        "za": flip_a(zh),
        "zb": flip_b(zh),
        "ya": flip_a(y),
        "yb": flip_b(y),
        "zz": (zh + 2) % 4,
        "yy": (y + 2) % 4,
    }
    to_x = (zh % 2) * 2 + y // 2
    to_z = (zh + 2 + to_x + 4 - x) % 4
    to_y = y + zl * (flip_b(y) - y)
    dest = device(to_z, to_y, core, zh // 2, to_x)
    dest_slot = storage(to_z, to_y, core)
    from_z = zl * 2 + x // 2
    from_l = (y // 2 + x % 2) % 2
    from_y = y + from_l * (flip_b(y) - y)
    source = device(from_z, from_y, core, from_l, (from_z + 2 + x + 4 - zh) % 4)
    is_self = (dest[0] == row) & (dest[1] == col)
    not_self = jnp.logical_not(is_self)

    HALF = ROWS // 2
    loads = [
        pltpu.make_async_copy(
            m_hbm.at[pl.ds(n * HALF, HALF)], m_ref.at[pl.ds(n * HALF, HALF)], load_sem.at[n]
        )
        for n in range(2)
    ]
    for c in loads:
        c.start()

    barrier = pltpu.get_barrier_semaphore()

    def greet(dev):
        pl.semaphore_signal(barrier, inc=1, device_id=dev, device_id_type=MESH)

    for dev in partner.values():
        greet(dev)

    @pl.when(not_self)
    def _():
        greet(dest)
        greet(source)

    ids = {}
    sent = []

    def copy(key, src, dst, dev):
        n = ids.setdefault(key, len(ids))
        return pltpu.make_async_remote_copy(
            src_ref=src,
            dst_ref=dst,
            send_sem=send_sem.at[n],
            recv_sem=recv_sem.at[n],
            device_id=dev,
            device_id_type=MESH,
        )

    def send(key, src, dst, dim):
        c = copy(key, src, dst, partner[dim])
        c.start()
        sent.append(c)

    def arrive(key, dst, dim):
        copy(key, dst, dst, partner[dim]).wait_recv()

    def at(ref, p, start, size):
        return ref.at[p, pl.ds(pl.multiple_of(start, 8), size), :]

    def load(ref, p, start, size):
        return ref[p, pl.ds(pl.multiple_of(start, 8), size), :]

    PAIR = 2 * PIECE
    across_x = (("xa", flip_a(x)), ("xb", flip_b(x)), ("xf", (x + 2) % 4))

    def rx_at(p, n):
        return rx.at[p, n * PAIR : (n + 1) * PAIR, :]

    def last(p):
        return rx.at[p, 3 * PAIR :, :]

    def scatter_one(p):
        for n, (d, x_) in enumerate(across_x):
            send(("rs0", p, d), at(s_ref, p, x_ * PAIR, PAIR), rx_at(p, n), d)

    def scatter_two(p):
        for n, (d, _) in enumerate(across_x):
            arrive(("rs0", p, d), rx_at(p, n), d)
        near = load(s_ref, p, x * PAIR, PAIR) + rx[p, :PAIR, :]
        far = rx[p, PAIR : 2 * PAIR, :] + rx[p, 2 * PAIR : 3 * PAIR, :]
        sum_one[p] = near + far
        send(("rs1", p), at(sum_one, p, (1 - zl) * PIECE, PIECE), last(p), "zl")

    def scattered(p):
        arrive(("rs1", p), last(p), "zl")
        return load(sum_one, p, zl * PIECE, PIECE) + rx[p, 3 * PAIR :, :]

    def corner_one():
        d = ORDERS[CORNER][0]
        send(("k", 0), at(s_ref, CORNER, (1 - bits[d]) * 256, 256), rx.at[CORNER, :256], d)

    def corner_two():
        d, e = ORDERS[CORNER][:2]
        arrive(("k", 0), rx.at[CORNER, :256], d)
        half[...] = load(s_ref, CORNER, bits[d] * 256, 256) + rx[CORNER, :256]
        start = pl.multiple_of((1 - bits[e]) * 128, 8)
        send(("k", 1), half.at[pl.ds(start, 128)], rx.at[CORNER, 256:384], e)

    def corner_three():
        d, e = ORDERS[CORNER][1:]
        arrive(("k", 1), rx.at[CORNER, 256:384], d)
        kept = half[pl.ds(pl.multiple_of(bits[d] * 128, 8), 128)]
        sum_one[CORNER] = kept + rx[CORNER, 256:384]
        send(("k", 2), at(sum_one, CORNER, (1 - bits[e]) * 64, 64), rx.at[CORNER, 384:448], e)

    mine = storage(zh, y, core)

    def c_at(p, slot, count):
        return at(c_ref, p, slot * PIECE, count * PIECE)

    def place(p):
        return copy(("place", p), q.at[p], c_at(p, dest_slot, 1), dest)

    def keep(p):
        return pltpu.make_async_copy(q.at[p], c_at(p, dest_slot, 1), own_sem.at[p])

    def my_slot(p):
        a, b, c = ORDERS[p]
        return bits[a] * 4 + bits[b] * 2 + bits[c]

    def r_at(p, slot, count):
        return at(r_ref, p, slot * PIECE, count * PIECE)

    def place_part(p):
        q[p] = scattered(p)

        @pl.when(not_self)
        def _():
            place(p).start()

        @pl.when(is_self)
        def _():
            keep(p).start()

        r_ref[p, pl.ds(pl.multiple_of(my_slot(p) * PIECE, 8), PIECE), :] = q[p]
        send(("r0", p), q.at[p], r_at(p, my_slot(p), 1), ORDERS[p][2])

    def row_two(p):
        a, b, c = ORDERS[p]
        arrive(("r0", p), r_at(p, bits[a] * 4 + bits[b] * 2 + 1 - bits[c], 1), c)
        pair = bits[a] * 4 + bits[b] * 2
        send(("r1", p), r_at(p, pair, 2), r_at(p, pair, 2), b)

    def row_three(p):
        a, b, c = ORDERS[p]
        arrive(("r1", p), r_at(p, bits[a] * 4 + (1 - bits[b]) * 2, 2), b)
        send(("r2", p), r_at(p, bits[a] * 4, 4), r_at(p, bits[a] * 4, 4), a)

    def row_done(p):
        a = ORDERS[p][0]
        arrive(("r2", p), r_at(p, (1 - bits[a]) * 4, 4), a)

    def corner_send(n):
        for m, d in enumerate(CORNER_SUM[n]):
            send(("ar", n, d), ar.at[n], arx.at[3 * n + m], d)

    def corner_add(n):
        total = ar[n]
        for m, d in enumerate(CORNER_SUM[n]):
            arrive(("ar", n, d), arx.at[3 * n + m], d)
            total = total + arx[3 * n + m]
        ar[n + 1] = total

    def corner_start():
        d = ORDERS[CORNER][2]
        arrive(("k", 2), rx.at[CORNER, 384:448], d)
        ar[0] = load(sum_one, CORNER, bits[d] * 64, 64) + rx[CORNER, 384:448]
        corner_send(0)

    def corner_step(n):
        corner_add(n - 1)
        corner_send(n)

    def corner_gather(n):
        slot = x * 2 + zl
        if n == 0:
            corner_add(2)
            k_ref[pl.ds(slot, 1)] = ar[3][None]
            send(("g0",), ar.at[3], k_ref.at[slot], "zl")
        if n == 1:
            arrive(("g0",), k_ref.at[x * 2 + 1 - zl], "zl")
            two = k_ref.at[pl.ds(x * 2, 2)]
            for d, _ in across_x:
                send(("g1", d), two, two, d)
        if n == 2:
            for d, x_ in across_x:
                arrive(("g1", d), k_ref.at[pl.ds(x_ * 2, 2)], d)

    def level(p, n):
        z0, z1 = Z_ORDERS[p]
        return (zh, flipped[z0], flipped[z1], flipped["zz"])[n]

    def spread(p, n):
        y0, y1 = Y_ORDERS[p]
        slot = c_at(p, storage(level(p, n), y, core), 1)
        send(("y0", p, n), slot, slot, y0)
        send(("y1", p, n), slot, slot, y1)

    def placed(p):
        @pl.when(not_self)
        def _():
            copy(("place", p), c_at(p, mine, 1), c_at(p, mine, 1), source).wait_recv()

        @pl.when(is_self)
        def _():
            keep(p).wait()

        z0, z1 = Z_ORDERS[p]
        send(("z0", p), c_at(p, mine, 1), c_at(p, mine, 1), z0)
        send(("z1", p), c_at(p, mine, 1), c_at(p, mine, 1), z1)
        spread(p, 0)

    def near_z(p):
        z0, z1 = Z_ORDERS[p]
        slot = c_at(p, storage(level(p, 1), y, core), 1)
        arrive(("z0", p), slot, z0)
        send(("z2", p), slot, slot, z1)
        spread(p, 1)
        arrive(("z1", p), c_at(p, storage(level(p, 2), y, core), 1), z1)
        spread(p, 2)

    def far_z(p):
        z1 = Z_ORDERS[p][1]
        arrive(("z2", p), c_at(p, storage(level(p, 3), y, core), 1), z1)
        spread(p, 3)
        share(p, 0, y)

    def share(p, n, y_):
        block = c_at(p, storage(0, y_, core), 4)
        send(("c", p, n), block, block, "co")

    def near_y(p, n):
        y0, y1 = Y_ORDERS[p]
        slot = c_at(p, storage(level(p, n), flipped[y0], core), 1)
        arrive(("y0", p, n), slot, y0)
        send(("y2", p, n), slot, slot, y1)

    def next_y(p):
        y1 = Y_ORDERS[p][1]
        for n in range(4):
            arrive(("y1", p, n), c_at(p, storage(level(p, n), flipped[y1], core), 1), y1)
        share(p, 2, flipped[y1])

    def far_y(p):
        y1 = Y_ORDERS[p][1]
        for n in range(4):
            arrive(("y2", p, n), c_at(p, storage(level(p, n), flipped["yy"], core), 1), y1)
        share(p, 3, flipped["yy"])

    def shared(p, n):
        y0, y1 = Y_ORDERS[p]
        y_ = (y, flipped[y0], flipped[y1], flipped["yy"])[n]
        arrive(("c", p, n), c_at(p, storage(0, y_, 1 - core), 4), "co")

    pivots = pivots_ref[...]
    row_start, col_start = row * ROWS, col * COLS

    def choose(h):
        places = lax.broadcasted_iota(jnp.int32, (COLS, NB), 0) + col_start
        onehot[...] = (places == pivots[:, h * NB : (h + 1) * NB]).astype(F32).astype(BF16)
        corner = None
        for n in range(2):
            if h == 0:
                loads[n].wait()
            hi, lo = split(m_ref[n * HALF : (n + 1) * HALF, :])
            picked = dot(hi, onehot[...], NN) + dot(lo, onehot[...], NN)
            for g in range(2):
                p = 2 * h + g
                for s in range(4 * n, 4 * n + 4):
                    slot = source_slot(s) * PIECE
                    s_ref[p, slot : slot + PIECE, :] = picked[
                        s * PIECE - n * HALF : (s + 1) * PIECE - n * HALF,
                        g * LANES : (g + 1) * LANES,
                    ]
            if h == 0:
                places = lax.broadcasted_iota(jnp.int32, (HALF, NB), 0) + (row_start + n * HALF)
                chosen = (places == pivots[:, NB:]).astype(F32).astype(BF16)
                hi, lo = split(picked)
                term = dot(chosen, hi, TN) + dot(chosen, lo, TN)
                corner = term if corner is None else corner + term
        return corner

    corner = choose(0)

    @pl.when(not_self)
    def _():
        pl.semaphore_wait(barrier, len(partner) + 2)

    @pl.when(is_self)
    def _():
        pl.semaphore_wait(barrier, len(partner))

    scatter_one(0)
    for s in range(8):
        slot = slot_of(ORDERS[CORNER], s) * PIECE
        for g in range(2):
            s_ref[CORNER, slot + g * 32 : slot + (g + 1) * 32, :] = corner[
                s * 32 : (s + 1) * 32, g * LANES : (g + 1) * LANES
            ]
    corner_one()
    scatter_one(1)
    choose(1)
    corner_two()
    scatter_one(2)
    scatter_two(0)
    corner_three()
    scatter_one(3)
    place_part(0)
    scatter_two(1)
    corner_start()
    place_part(1)
    placed(0)
    scatter_two(2)
    corner_step(1)
    near_z(0)
    place_part(2)
    near_y(0, 0)
    placed(1)
    scatter_two(3)
    near_y(0, 1)
    near_y(0, 2)
    far_z(0)
    near_z(1)
    place_part(3)
    placed(2)
    near_y(1, 0)
    corner_step(2)
    row_two(0)
    row_two(1)
    near_y(0, 3)
    share(0, 1, flipped[Y_ORDERS[0][0]])
    near_y(1, 1)
    near_y(1, 2)
    far_z(1)
    near_z(2)
    corner_gather(0)
    placed(3)
    near_y(2, 0)
    row_two(2)
    row_two(3)
    corner_gather(1)
    near_y(1, 3)
    share(1, 1, flipped[Y_ORDERS[1][0]])
    far_z(2)
    near_z(3)
    near_y(2, 1)
    near_y(2, 2)
    row_three(0)
    row_three(1)
    near_y(3, 0)
    far_z(3)
    near_y(2, 3)
    share(2, 1, flipped[Y_ORDERS[2][0]])
    row_three(2)
    row_three(3)
    near_y(3, 1)
    near_y(3, 2)
    near_y(3, 3)
    share(3, 1, flipped[Y_ORDERS[3][0]])
    corner_gather(2)
    for p in range(PARTS):
        row_done(p)

    slots = [source_slot(s) for s in range(8)]
    corner = jnp.concatenate(
        [
            jnp.concatenate([k_ref[slot, :32, :], k_ref[slot, 32:, :]], axis=1)
            for slot in slots
        ],
        axis=0,
    )
    w_one, w_two = split(w_ref[0]), split(w_ref[1])
    t = split(dot3(w_one, split(corner), NT))
    t_hi[...], t_lo[...] = t
    rows = [
        jnp.concatenate(
            [
                r_ref[p, slot * PIECE : (slot + 1) * PIECE, :]
                for slot in (slot_of(ORDERS[p], s) for s in range(8))
            ],
            axis=0,
        )
        for p in range(PARTS)
    ]
    row_ids = row_start + lax.broadcasted_iota(jnp.int32, (ROWS, NB), 0)
    live_one = live(row_ids, pivots[:, :NB])
    live_two = live_one * live(row_ids, pivots[:, NB:])
    one = split(jnp.concatenate(rows[:2], axis=1))
    factor_one = live_one * dot3(one, w_one, NN)
    two = jnp.concatenate(rows[2:], axis=1) - live_one * dot3(one, t, NN)
    factor_two = live_two * dot3(split(two), w_two, NN)
    factor_ref[:, :NB] = factor_one
    factor_ref[:, NB:] = factor_two
    left_hi[:, :NB], left_lo[:, :NB] = split(factor_one)
    left_hi[:, NB:], left_lo[:, NB:] = split(factor_two)

    def update(y_, core_):
        over = (y_ // 2 + x % 2) % 2
        y_from = y_ + over * (flip_b(y_) - y_)
        start = ((y_from % 2) * 2 + core_) * 512 + over * 256
        first = [
            storage((from_z + 2 + x + 4 - s) % 4, y_, core_) * PIECE for s in range(4)
        ]
        piece = [
            jnp.concatenate([load(c_ref, p, f, PIECE) for f in first], axis=0)
            for p in range(PARTS)
        ]
        place_ = lax.broadcasted_iota(jnp.int32, (4 * PIECE, NB), 0)
        place_ = place_ + (col_start + start)
        live_one = live(place_, pivots[:, :NB])
        live_two = live_one * live(place_, pivots[:, NB:])
        one = live_one * jnp.concatenate(piece[:2], axis=1)
        one_hi, one_lo = split(one)
        two = jnp.concatenate(piece[2:], axis=1)
        two = live_two * (two - dot3((one_hi, one_lo), (t_hi[...], t_lo[...]), NN))
        two_hi, two_lo = split(two)
        right = (
            jnp.concatenate([one_hi, two_hi], axis=1),
            jnp.concatenate([one_lo, two_lo], axis=1),
        )
        term = dot3((left_hi[...], left_lo[...]), right, NT)
        columns = pl.ds(pl.multiple_of(start, NB), NB)
        out_ref[:, columns] = m_ref[:, columns] - term

    for p in range(PARTS):
        next_y(p)
    update(y, core)
    for p in range(PARTS):
        shared(p, 0)
    update(y, 1 - core)
    update(flipped["ya"], core)
    for p in range(PARTS):
        far_y(p)
    update(flipped["yb"], core)
    for p in range(PARTS):
        shared(p, 1)
        shared(p, 2)
    update(flipped["ya"], 1 - core)
    update(flipped["yb"], 1 - core)
    update(flipped["yy"], core)
    for p in range(PARTS):
        shared(p, 3)
    update(flipped["yy"], 1 - core)

    @pl.when(not_self)
    def _():
        for p in range(PARTS):
            place(p).wait_send()

    for c in sent:
        c.wait_send()
    assert len(ids) == MESSAGES, len(ids)


MESSAGES = (4 + 1 + 3 + 12 + 4 + 3) * PARTS + 3 + 7 + 4


def shards(matrix, inverse_blocks, pivots):
    vmem = pl.BlockSpec(memory_space=pltpu.VMEM)

    def panel(rows):
        return pltpu.VMEM((PARTS + 1, rows, LANES), F32)

    return tuple(
        pl.pallas_call(
            panels_kernel,
            name="panels",
            out_shape=(
                jax.ShapeDtypeStruct((ROWS, COLS), F32),
                jax.ShapeDtypeStruct((ROWS, NP), F32),
            ),
            in_specs=[vmem, vmem, pl.BlockSpec(memory_space=pltpu.HBM)],
            out_specs=(vmem, vmem),
            scratch_shapes=[
                pltpu.VMEM((ROWS, COLS), F32),
                pltpu.VMEM((COLS, NB), BF16),
                panel(8 * PIECE),
                panel(7 * PIECE),
                panel(2 * PIECE),
                pltpu.VMEM((4 * PIECE, LANES), F32),
                pltpu.VMEM((PARTS, PIECE, LANES), F32),
                pltpu.VMEM((PARTS, COLS, LANES), F32),
                pltpu.VMEM((PARTS, ROWS, LANES), F32),
                pltpu.VMEM((8, PIECE, LANES), F32),
                pltpu.VMEM((4, PIECE, LANES), F32),
                pltpu.VMEM((7, PIECE, LANES), F32),
                pltpu.VMEM((ROWS, NP), BF16),
                pltpu.VMEM((ROWS, NP), BF16),
                pltpu.VMEM((NB, NB), BF16),
                pltpu.VMEM((NB, NB), BF16),
                pltpu.SemaphoreType.DMA((MESSAGES,)),
                pltpu.SemaphoreType.DMA((MESSAGES,)),
                pltpu.SemaphoreType.DMA((PARTS,)),
                pltpu.SemaphoreType.DMA((2,)),
            ],
            compiler_params=pltpu.CompilerParams(
                collective_id=0, has_side_effects=True, vmem_limit_bytes=48 << 20
            ),
        )(pivots.reshape(1, NP), inverse_blocks, matrix)
    )


def solution(mesh):
    return jax.shard_map(
        shards,
        mesh=mesh,
        in_specs=(P("row", "col"), P(), P()),
        out_specs=(P("row", "col"), P("row", None)),
        check_vma=False,
    )
```
